32 devices in a mesh: groups: 2 (over x), wide: 16 (over z, y, core).
Axes of the slice: x: 2, y: 2, z: 4, core: 2. Of those that a mesh axis runs over, the one named last changes fastest.
Arguments:
- queries: bfloat16 [32, 16, 8, 128], P(('groups', 'wide')), parts along dimension 0, may hold values from -250 to 250
- keys_cache: bfloat16 [32, 16, 320, 128], P(('groups', 'wide')), parts along dimension 0, may hold values from -6 to 6
- values_cache: bfloat16 [32, 16, 320, 128], P(('groups', 'wide')), parts along dimension 0, may hold values from -6 to 6
- new_keys: bfloat16 [32, 16, 128], P(('groups', 'wide')), parts along dimension 0, may hold values from -6 to 6
- new_values: bfloat16 [32, 16, 128], P(('groups', 'wide')), parts along dimension 0, may hold values from -6 to 6
- lengths: int32 [64], P('groups'), parts along dimension 0, may hold values from 1 to 320, as said below
- assignment: int32 [64], P('groups'), parts along dimension 0, may hold values from 0 to 31, each once
- residual: bfloat16 [64, 8192], P('groups', 'wide'), parts along dimension 0, may hold values from -6 to 6
- w_out: bfloat16 [8192, 8192], P('wide'), may hold values from -0.0625 to 0.0625
- w_gate: bfloat16 [20480, 8192], P('wide'), may hold values from -0.0625 to 0.0625
- w_up: bfloat16 [20480, 8192], P('wide'), may hold values from -0.0625 to 0.0625
- w_down: bfloat16 [20480, 8192], P('wide'), may hold values from -0.0625 to 0.0625
- norm_gain: float32 [8192], P('wide'), may hold values from 0.25 to 1.75
Outputs:
- mixed: bfloat16 [64, 8192], P('groups', 'wide'), parts along dimension 0
The draws below stay inside these ranges and needn't reach their ends.
There are 2 independent parts, one for each index of `groups`. The reference program is written for one: setup_inputs(seed, part) draws one part's arguments, and reference() takes and returns one part's arrays. A program takes and returns all parts, laid end to end along the dimension named above; an argument that names none is the same for every part. Nothing has to cross between parts.
Inputs may be any that keep to these rules, and one draw needn't show every extreme that they name: `lengths`: every length is at least 1; one cache row has length exactly 320 in every draw. `assignment`: A permutation of the request numbers.
All inputs are finite; a program needn't handle non-finite values.
Results may differ from the reference program's by a relative error of at most 0.0052.
Values may be sent and summed in bfloat16 or wider, within the bound.
No kernel may reach another device: no remote copies, remote signals or barrier semaphores. Data moves between devices by JAX's collectives and lax.ppermute only.
A program may use at most 128 MiB of HBM per device.

```python
import jax
import jax.numpy as jnp
from jax import lax

D = 8192
KV = 8
QPK = 8
HEAD = 128
FF = 20480
REQ_DEV = 16
LEN = 320
SHARDS = 2
SLOTS = 16
REQUESTS = 32


def draw_lengths(key, part):
    shard_caps = jax.random.randint(jax.random.fold_in(key, 11), (SHARDS,), LEN // 4, LEN + 1)
    raw_draw = jax.random.randint(jax.random.fold_in(key, 12), (SHARDS, REQ_DEV), 0, 1 << 20)
    drawn_lengths = (raw_draw % shard_caps[:, None] + 1).reshape(SHARDS * REQ_DEV)
    chosen_row = jax.random.randint(jax.random.fold_in(key, 13), (), 0, SHARDS * REQ_DEV)
    row_number = jnp.arange(SHARDS * REQ_DEV, dtype=jnp.int32)
    return jnp.where(row_number == chosen_row, LEN, drawn_lengths).astype(jnp.int32)


def draw_queries(key, part):
    drawn_values = jax.random.normal(key, (SLOTS, REQ_DEV, QPK, HEAD), jnp.float32)
    drawn_values = jnp.clip(drawn_values, -6.0, 6.0)
    return drawn_values.astype(jnp.bfloat16)


def with_spikes(drawn, stream_key, source, target, shards_of, factor):
    owner, partner = [(jnp.arange(drawn.shape[dim]) // (drawn.shape[dim] // shards_of)).reshape([-1 if axis == dim else 1 for axis in range(drawn.ndim)]) for dim in (source, target)]
    chosen = jax.random.permutation(stream_key, shards_of)[partner]
    strong = (owner == chosen) | (owner == (partner + shards_of // 2) % shards_of)
    return jnp.where(strong, factor * drawn, drawn)


def block_levels(own_key, dims, cuts, low, high):
    gain = 1.0
    for dim, shards_of in cuts:
        heights = jax.random.uniform(jax.random.fold_in(jax.random.fold_in(own_key, 6), dim), (shards_of,), jnp.float32, low / len(cuts), high / len(cuts))
        gain = gain * jnp.repeat(jnp.exp(heights), dims[dim] // shards_of).reshape((-1,) + (1,) * (len(dims) - 1 - dim))
    return gain


def normal_values(key, shape, scale, most, shards=(), kind=jnp.bfloat16):
    drawn = jax.random.normal(key, shape, jnp.float32) * scale
    if len(shards) > 0:
        drawn = block_levels(key, shape, shards, -0.22, 0.18) * drawn
    return jnp.clip(drawn, min=-most, max=most).astype(kind)


def heavy_noise(stream_key, shape, scale, most, shards, heavy, kind=jnp.bfloat16):
    entries = scale * jax.random.normal(stream_key, shape, jnp.float32)
    if shards:
        entries = entries * block_levels(stream_key, shape, shards, -0.22, 0.18)
    return jnp.clip(with_spikes(entries, jax.random.fold_in(stream_key, 3), *heavy), -most, most).astype(kind)


def setup_inputs(seed: int = 0, part: int = 0) -> dict:
    seeds = jax.random.split(jax.random.key(seed), 14)
    own_keys = jax.random.split(jax.random.fold_in(seeds[13], part), 14)
    queries = draw_queries(jax.random.fold_in(jax.random.fold_in(seeds[13], part), 71), part)
    keys_cache = normal_values(own_keys[1], (SLOTS, REQ_DEV, LEN, HEAD), 1.0, 6.0, ((0, 16),))
    values_cache = normal_values(own_keys[2], (SLOTS, REQ_DEV, LEN, HEAD), 1.0, 6.0, ((0, 16),))
    new_keys = normal_values(own_keys[3], (SLOTS, REQ_DEV, HEAD), 1.0, 6.0, ((0, 16),))
    new_values = normal_values(own_keys[4], (SLOTS, REQ_DEV, HEAD), 1.0, 6.0, ((0, 16),))
    lengths = draw_lengths(jax.random.fold_in(jax.random.fold_in(seeds[13], part), 71), part)
    assignment = jax.random.permutation(own_keys[6], REQUESTS).astype(jnp.int32)
    residual = normal_values(own_keys[7], (REQUESTS, D), 1.0, 6.0, ((1, 16),))
    w_out = normal_values(seeds[8], (D, D), D ** -0.5, 0.0625, ((0, 16),))
    w_gate = normal_values(seeds[9], (FF, D), D ** -0.5, 0.0625, ((0, 16),))
    w_up = normal_values(seeds[10], (FF, D), D ** -0.5, 0.0625, ((0, 16),))
    w_down = heavy_noise(seeds[11], (FF, D), FF ** -0.5, 0.0625, ((0, 16),), (0, 1, 16, 2.0))
    norm_gain = jnp.clip(1.0 + 0.15 * jax.random.normal(seeds[12], (D,), jnp.float32), 0.25, 1.75)
    return dict(queries=queries, keys_cache=keys_cache, values_cache=values_cache, new_keys=new_keys, new_values=new_values, lengths=lengths, assignment=assignment, residual=residual, w_out=w_out, w_gate=w_gate, w_up=w_up, w_down=w_down, norm_gain=norm_gain)


def attend_slot(query_rows, keys_local, values_local, key_new, value_new, lens_local):
    inv_scale = HEAD ** (-0.5)
    scores = jnp.einsum('rqe,rpe->rqp', query_rows.astype(jnp.float32), keys_local.astype(jnp.float32)) * inv_scale
    position = jnp.arange(LEN, dtype=jnp.int32)
    scores = jnp.where(position[None, None, :] < lens_local[:, None, None], scores, -1e+30)
    own_score = jnp.einsum('rqe,re->rq', query_rows.astype(jnp.float32), key_new.astype(jnp.float32)) * inv_scale
    top_score = jnp.maximum(lax.optimization_barrier(jnp.max(scores, axis=2)), own_score)
    weights = jnp.exp(scores - top_score[:, :, None])
    own_weight = jnp.exp(own_score - top_score)
    total_sum = lax.optimization_barrier(jnp.sum(weights, axis=2)) + own_weight
    weights_low = lax.optimization_barrier(weights.astype(jnp.bfloat16)).astype(jnp.float32)
    own_low = lax.optimization_barrier(own_weight.astype(jnp.bfloat16)).astype(jnp.float32)
    weighted = jnp.einsum('rqp,rpe->rqe', weights_low, values_local.astype(jnp.float32))
    weighted = weighted + own_low[:, :, None] * value_new.astype(jnp.float32)[:, None, :]
    return (weighted / total_sum[:, :, None]).astype(jnp.bfloat16).reshape(REQ_DEV, QPK * HEAD)

def contract_last(left, right):
    return lax.dot_general(left, right, (((1,), (1,)), ((), ())), preferred_element_type=jnp.float32)

def reference(queries, keys_cache, values_cache, new_keys, new_values, lengths, assignment, residual, w_out, w_gate, w_up, w_down, norm_gain):
    slot_lengths = jnp.broadcast_to(lengths.reshape(SHARDS, 1, REQ_DEV), (SHARDS, KV, REQ_DEV)).reshape(SLOTS, REQ_DEV)
    per_slot = lax.map(lambda items: attend_slot(*items), (queries, keys_cache, values_cache, new_keys, new_values, slot_lengths))
    attended = per_slot.reshape(SHARDS, KV, REQ_DEV, QPK * HEAD).transpose(0, 2, 1, 3).reshape(REQUESTS, D)
    by_request = jnp.zeros((REQUESTS, D), jnp.bfloat16).at[assignment.astype(jnp.int32)].set(attended)
    state = residual.astype(jnp.float32) + contract_last(by_request, w_out)
    inv_rms = lax.rsqrt(lax.optimization_barrier(jnp.mean(state * state, axis=1)) + 1e-05)
    normed = (state * inv_rms[:, None] * norm_gain[None, :]).astype(jnp.bfloat16)
    gate_val = contract_last(normed, w_gate)
    up_val = contract_last(normed, w_up)
    hidden = (jax.nn.silu(gate_val) * up_val).astype(jnp.bfloat16)
    return (state + jnp.dot(hidden, w_down, preferred_element_type=jnp.float32)).astype(jnp.bfloat16)
```

```python
import functools
import math

import jax
import jax.numpy as jnp
from jax import lax
from jax.experimental import pallas as pl
from jax.experimental.pallas import tpu as pltpu
from jax.sharding import PartitionSpec as P

KEY_BLOCK = 64
EPSILON = 1e-05
NEG_FILL = -1e30
ROWS = 256
LANES = 128
CACHE_CUTS = 4
DOWN_SLOTS = 2
DOWN_AHEAD = 2


HBM = pl.BlockSpec(memory_space=pltpu.HBM)
VMEM = pl.BlockSpec(memory_space=pltpu.VMEM)
SMEM = pl.BlockSpec(memory_space=pltpu.SMEM)
ANY = pl.BlockSpec(memory_space=pl.ANY)
DMA = pltpu.SemaphoreType.DMA


def contract_last(left, right):
    return lax.dot_general(
        left, right, (((1,), (1,)), ((), ())), preferred_element_type=jnp.float32
    )


def vmem_out(shape, dtype):
    return pltpu.VMEM(tuple(shape), dtype)


def params(mib):
    return pltpu.CompilerParams(vmem_limit_bytes=mib << 20)


def cost(flops, moved):
    return pl.CostEstimate(flops=int(flops), bytes_accessed=int(moved), transcendentals=0)


def in_hbm(array):
    return pltpu.with_memory_space_constraint(array, pltpu.HBM)


def in_vmem(array):
    return pltpu.with_memory_space_constraint(array, pltpu.VMEM)


def piece_copy(weights, index, piece, sem):
    return pltpu.make_async_copy(weights.at[pl.ds(index * ROWS, ROWS)], piece, sem)


def prefetch_kernel(plan, sources, deps, *refs):
    weights = refs[:sources]
    pieces, sems = refs[sources + deps : -1], refs[-1]
    copies = [
        piece_copy(weights[which], index, pieces[i], sems.at[i])
        for i, (which, index) in enumerate(plan)
    ]
    for copy in copies:
        copy.start()
    for copy in copies:
        copy.wait()


def prefetch(weights, plan, deps):
    width = weights[0].shape[1]
    return pl.pallas_call(
        functools.partial(prefetch_kernel, plan, len(weights), len(deps)),
        out_shape=[vmem_out((ROWS, width), weights[0].dtype) for _ in plan],
        in_specs=[HBM] * len(weights) + [ANY] * len(deps),
        out_specs=[VMEM] * len(plan),
        scratch_shapes=[DMA((len(plan),))],
        compiler_params=params(1),
        cost_estimate=cost(0, len(plan) * ROWS * width * 2),
        name="prefetch",
    )(*map(in_hbm, weights), *deps)


def attention_kernel(kv_heads, meta, lens, q, nk, nv, k_hbm, v_hbm, wo_hbm, att, wo, kb, vb, rows_f32, sk, sv, sw):
    count, heads, head = q.shape
    positions = kb.shape[1]
    cut = count // CACHE_CUTS
    copies = []
    for c in range(CACHE_CUTS):
        part = pl.ds(c * cut, cut)
        copies.append(
            (
                pltpu.make_async_copy(k_hbm.at[part], kb.at[part], sk.at[c]),
                pltpu.make_async_copy(v_hbm.at[part], vb.at[part], sv.at[c]),
            )
        )
    fetch = pltpu.make_async_copy(wo_hbm, wo, sw)
    for pair in copies:
        for copy in pair:
            copy.start()
    fetch.start()
    base = (meta[0] // kv_heads) * count
    scale = 1.0 / math.sqrt(head)
    position = lax.broadcasted_iota(jnp.int32, (heads, positions), 1)
    for c in range(CACHE_CUTS):
        for copy in copies[c]:
            copy.wait()
        for r in range(c * cut, (c + 1) * cut):
            query = q[r]
            score = contract_last(query, kb[r]) * scale
            score = jnp.where(position < lens[base + r], score, NEG_FILL)
            own = (
                jnp.sum(
                    query.astype(jnp.float32) * nk[r : r + 1].astype(jnp.float32),
                    axis=1,
                    keepdims=True,
                )
                * scale
            )
            top = jnp.maximum(jnp.max(score, axis=1, keepdims=True), own)
            weight = jnp.exp(score - top)
            own_weight = jnp.exp(own - top)
            total = jnp.sum(weight, axis=1, keepdims=True) + own_weight
            mixed = jnp.dot(
                weight.astype(jnp.bfloat16), vb[r], preferred_element_type=jnp.float32
            )
            own_low = own_weight.astype(jnp.bfloat16).astype(jnp.float32)
            mixed = mixed + own_low * nv[r : r + 1].astype(jnp.float32)
            rows_f32[r * heads : (r + 1) * heads, :] = mixed / total
    for h in range(heads):
        att[:, h * head : (h + 1) * head] = rows_f32[pl.ds(h, count, stride=heads), :].astype(
            att.dtype
        )
    fetch.wait()


def attention(meta, lengths, q, k, v, nk, nv, w_out, kv_heads):
    count, heads, head = q.shape
    return pl.pallas_call(
        functools.partial(attention_kernel, kv_heads),
        out_shape=[
            vmem_out((count, heads * head), jnp.bfloat16),
            vmem_out(w_out.shape, w_out.dtype),
        ],
        in_specs=[SMEM, SMEM, VMEM, VMEM, VMEM, HBM, HBM, HBM],
        out_specs=[VMEM, VMEM],
        scratch_shapes=[
            pltpu.VMEM(k.shape, k.dtype),
            pltpu.VMEM(v.shape, v.dtype),
            pltpu.VMEM((count * heads, head), jnp.float32),
            DMA((CACHE_CUTS,)),
            DMA((CACHE_CUTS,)),
            DMA,
        ],
        compiler_params=params(4),
        cost_estimate=cost(0, 2 * w_out.size),
        name="attention",
    )(meta, lengths, q, nk, nv, in_hbm(k), in_hbm(v), in_hbm(w_out))


def stack_kernel(count, *refs):
    out = refs[-1]
    for i in range(count):
        out[i] = refs[i][...]


def stack(blocks, deps):
    return pl.pallas_call(
        functools.partial(stack_kernel, len(blocks)),
        out_shape=vmem_out((len(blocks),) + blocks[0].shape, blocks[0].dtype),
        in_specs=[VMEM] * len(blocks) + [ANY] * len(deps),
        out_specs=VMEM,
        compiler_params=params(1),
        name="stack",
    )(*blocks, *deps)


def swap(value, size, bit):
    return lax.ppermute(value, "wide", [(i, i ^ bit) for i in range(size)])


def shift(value, size, step):
    return lax.ppermute(value, "wide", [(i, (i + step) % size) for i in range(size)])


def place(meta):
    mine = meta[0]
    return mine // 4, (mine // 2) % 2, mine % 2


def project_kernel(
    planes, kv_heads, plan, sources, deps, meta, b0, b1, c0, c1, wo, residual, rows_row, gain, *refs
):
    weights = refs[:sources]
    refs = refs[sources + deps :]
    pieces = refs[: len(plan)]
    state_ref, message, gathered, sems = refs[len(plan) :]
    copies = [
        piece_copy(weights[which], index, pieces[i], sems.at[i])
        for i, (which, index) in enumerate(plan)
    ]
    for copy in copies:
        copy.start()
    z, y, core = place(meta)
    count, width = b0.shape[1:]
    for block, yy, cc in ((b0, y, core), (c0, y, 1 - core), (b1, 1 - y, core), (c1, 1 - y, 1 - core)):
        for k in range(planes):
            source = lax.rem(z + planes - k, planes) * 4 + yy * 2 + cc
            row = pl.multiple_of((source // kv_heads) * count, count)
            lane = pl.multiple_of(lax.rem(source, kv_heads) * width, width)
            gathered[pl.ds(row, count), pl.ds(lane, width)] = block[k]
    requests, features = residual.shape
    numbers = lax.broadcasted_iota(jnp.int32, (requests, requests), 0)
    pick = (rows_row[...] == numbers).astype(jnp.bfloat16)
    squares = jnp.zeros((requests, 1), jnp.float32)
    for j in range(0, features, LANES * 2):
        cut = slice(j, min(j + LANES * 2, features))
        part = lax.dot_general(
            pick, residual[:, cut], (((0,), (0,)), ((), ())), preferred_element_type=jnp.float32
        )
        part = part + contract_last(gathered[...], wo[cut, :])
        state_ref[:, cut] = part
        message[:, cut] = (part * gain[:, cut]).astype(message.dtype)
        squares = squares + jnp.sum(part * part, axis=1, keepdims=True)
    high = squares.astype(jnp.bfloat16).astype(jnp.float32)
    low = squares - high
    lane = lax.broadcasted_iota(jnp.int32, (requests, LANES), 1)
    tail = jnp.where(lane == 0, high, jnp.where(lane == 1, low, 0.0))
    message[:, features:] = tail.astype(message.dtype)
    for copy in copies:
        copy.wait()


def project(meta, blocks, wo, residual, rows_row, gain, weights, plan, deps, planes, kv_heads):
    requests, features = residual.shape
    width = wo.shape[1]
    return pl.pallas_call(
        functools.partial(project_kernel, planes, kv_heads, plan, len(weights), len(deps)),
        out_shape=[vmem_out((ROWS, width), wo.dtype) for _ in plan]
        + [
            vmem_out((requests, features), jnp.float32),
            vmem_out((requests, features + LANES), jnp.bfloat16),
        ],
        in_specs=[SMEM] + [VMEM] * 8 + [HBM] * len(weights) + [ANY] * len(deps),
        out_specs=[VMEM] * (len(plan) + 2),
        scratch_shapes=[pltpu.VMEM((requests, width), jnp.bfloat16), DMA((max(len(plan), 1),))],
        compiler_params=params(4),
        cost_estimate=cost(0, wo.size * 2),
        name="project",
    )(meta, *blocks, in_vmem(wo), residual, rows_row, gain, *map(in_hbm, weights), *deps)


def half_inputs(z, core, planes, features, block, other, half):
    for k in range(planes):
        source = lax.rem(z + planes - k, planes)
        for part, cc in ((block, core), (other, 1 - core)):
            lane = pl.multiple_of((source * 2 + cc) * features, features)
            half[:, pl.ds(lane, features)] = part[k, :, :features]


def half_product(half, piece, planes, pair, yy):
    total = None
    for zz in range(planes):
        lane = pl.multiple_of((zz * 2 + yy) * pair, pair)
        term = contract_last(half[:, zz * pair : (zz + 1) * pair], piece[:, pl.ds(lane, pair)])
        total = term if total is None else total + term
    return total


def late_copies(weights, first, planes, pair, yy, late, sems):
    rows = pl.ds(first * ROWS, late.shape[0])
    copies = []
    for zz in range(planes):
        lane = pl.multiple_of((zz * 2 + yy) * pair, pair)
        copies.append(
            pltpu.make_async_copy(
                weights.at[rows, pl.ds(lane, pair)],
                late.at[:, pl.ds(zz * pair, pair)],
                sems.at[zz],
            )
        )
    return copies


def down_steps(planes):
    return [(dy, k) for dy in (1, 0) for k in range(planes)]


def down_copy(w_down, step, planes, z, y, pair, piece, sem):
    dy, k = down_steps(planes)[step]
    yy = 1 - y if dy else y
    lane = pl.multiple_of((lax.rem(z + k, planes) * 2 + yy) * pair, pair)
    return pltpu.make_async_copy(w_down.at[:, pl.ds(lane, pair)], piece, sem)


def first_half_kernel(planes, count, ready, meta, b0, c0, *refs):
    gates = refs[:count]
    ups = refs[count : count + ready]
    w_up, w_down = refs[count + ready : count + ready + 2]
    refs = refs[count + ready + 2 :]
    downs = refs[:DOWN_AHEAD]
    gate_sum, up_sum, half, late, late_sems, down_sems = refs[DOWN_AHEAD:]
    z, y, core = place(meta)
    features = b0.shape[2] - LANES
    pair = 2 * features
    copies = late_copies(w_up, ready, planes, pair, y, late, late_sems)
    ahead = [
        down_copy(w_down, i, planes, z, y, pair, downs[i], down_sems.at[i])
        for i in range(DOWN_AHEAD)
    ]
    for copy in copies + ahead:
        copy.start()
    half_inputs(z, core, planes, features, b0, c0, half)
    for j in range(count):
        gate_sum[:, j * ROWS : (j + 1) * ROWS] = half_product(half, gates[j], planes, pair, y)
    for j in range(ready):
        up_sum[:, j * ROWS : (j + 1) * ROWS] = half_product(half, ups[j], planes, pair, y)
    for copy in copies:
        copy.wait()
    for j in range(ready, count):
        rows = slice((j - ready) * ROWS, (j - ready + 1) * ROWS)
        up_sum[:, j * ROWS : (j + 1) * ROWS] = contract_last(half[...], late[rows, :])
    for copy in ahead:
        copy.wait()


def first_half(meta, b0, c0, gates, ups, w_up, w_down, planes):
    count, ready = len(gates), len(ups)
    requests = b0.shape[1]
    units, width = w_up.shape
    pair = 2 * (b0.shape[2] - LANES)
    return pl.pallas_call(
        functools.partial(first_half_kernel, planes, count, ready),
        out_shape=[vmem_out((units, pair), w_down.dtype) for _ in range(DOWN_AHEAD)]
        + [vmem_out((requests, units), jnp.float32)] * 2,
        in_specs=[SMEM] + [VMEM] * (2 + count + ready) + [HBM] * 2,
        out_specs=[VMEM] * (DOWN_AHEAD + 2),
        scratch_shapes=[
            pltpu.VMEM((requests, width // 2), jnp.bfloat16),
            pltpu.VMEM(((count - ready) * ROWS, width // 2), jnp.bfloat16),
            DMA((planes,)),
            DMA((DOWN_AHEAD,)),
        ],
        compiler_params=params(8),
        cost_estimate=cost(0, units * width * 2),
        name="first_half",
    )(meta, b0, c0, *map(in_vmem, gates), *map(in_vmem, ups), in_hbm(w_up), in_hbm(w_down))


def second_half_kernel(
    planes, count, ready, total_features, meta, b0, c0, b1, c1, gate_sum, up_sum, *refs
):
    gates, ups = refs[:count], refs[count : count + ready]
    downs = refs[count + ready : count + ready + DOWN_AHEAD]
    refs = refs[count + ready + DOWN_AHEAD :]
    w_up, w_down, keep, send, half, late, hidden, pieces, result, late_sems, down_sems = refs
    z, y, core = place(meta)
    features = b0.shape[2] - LANES
    pair = 2 * features
    order = down_steps(planes)

    def fetch(step):
        slot = step % DOWN_SLOTS
        return down_copy(w_down, step, planes, z, y, pair, pieces.at[slot], down_sems.at[slot])

    copies = late_copies(w_up, ready, planes, pair, 1 - y, late, late_sems)
    for copy in copies:
        copy.start()
    for step in range(DOWN_AHEAD, min(DOWN_AHEAD + DOWN_SLOTS, len(order))):
        fetch(step).start()
    squares = None
    for block in (b0, c0, b1, c1):
        for k in range(planes):
            term = block[k, :, features:].astype(jnp.float32)
            squares = term if squares is None else squares + term
    squares = jnp.sum(squares, axis=1, keepdims=True)
    inv_rms = lax.rsqrt(squares / total_features + EPSILON)
    half_inputs(z, core, planes, features, b1, c1, half)
    for j in range(count):
        cut = slice(j * ROWS, (j + 1) * ROWS)
        gate = gate_sum[:, cut] + half_product(half, gates[j], planes, pair, 1 - y)
        if j < ready:
            up = half_product(half, ups[j], planes, pair, 1 - y)
        else:
            if j == ready:
                for copy in copies:
                    copy.wait()
            up = contract_last(half[...], late[(j - ready) * ROWS : (j - ready + 1) * ROWS, :])
        up = (up_sum[:, cut] + up) * inv_rms
        gate = gate * inv_rms
        hidden[:, cut] = (gate * jax.nn.sigmoid(gate) * up).astype(hidden.dtype)
    mine = pl.ds(pl.multiple_of(core * features, features), features)
    other = pl.ds(pl.multiple_of((1 - core) * features, features), features)
    for step, (dy, k) in enumerate(order):
        spot = dy * planes + k
        if step < DOWN_AHEAD:
            piece = downs[step]
        else:
            fetch(step).wait()
            piece = pieces.at[step % DOWN_SLOTS]
        result[step % 2] = jnp.dot(hidden[...], piece[...], preferred_element_type=jnp.float32)
        keep[spot] = result[step % 2, :, mine]
        send[spot] = result[step % 2, :, other].astype(send.dtype)
        if step >= DOWN_AHEAD and step + DOWN_SLOTS < len(order):
            fetch(step + DOWN_SLOTS).start()


def second_half(meta, blocks, gate_sum, up_sum, gates, ups, downs, w_up, w_down, planes):
    count, ready = len(gates), len(ups)
    requests, units = gate_sum.shape
    width = w_down.shape[1]
    features = blocks[0].shape[2] - LANES
    return pl.pallas_call(
        functools.partial(second_half_kernel, planes, count, ready, width),
        out_shape=[
            vmem_out((2 * planes, requests, features), jnp.float32),
            vmem_out((2 * planes, requests, features), jnp.bfloat16),
        ],
        in_specs=[SMEM] + [VMEM] * (6 + count + ready + DOWN_AHEAD) + [HBM] * 2,
        out_specs=[VMEM] * 2,
        scratch_shapes=[
            pltpu.VMEM((requests, width // 2), jnp.bfloat16),
            pltpu.VMEM(((count - ready) * ROWS, width // 2), jnp.bfloat16),
            pltpu.VMEM((requests, units), jnp.bfloat16),
            pltpu.VMEM((DOWN_SLOTS, units, 2 * features), w_down.dtype),
            pltpu.VMEM((2, requests, 2 * features), jnp.float32),
            DMA((planes,)),
            DMA((DOWN_SLOTS,)),
        ],
        compiler_params=params(8 + (5 * DOWN_SLOTS + 1) // 2),
        cost_estimate=cost(0, 2 * units * width * 2),
        name="second_half",
    )(
        meta, *blocks, gate_sum, up_sum, *map(in_vmem, gates), *map(in_vmem, ups),
        *map(in_vmem, downs), in_hbm(w_up), in_hbm(w_down),
    )


def add_core_kernel(planes, keep, got, stay, send):
    for k in range(planes):
        send[k] = (keep[planes + k] + got[planes + k].astype(jnp.float32)).astype(send.dtype)
        stay[k] = keep[k] + got[k].astype(jnp.float32)


def add_core(keep, got, planes):
    shape = keep.shape[1:]
    return pl.pallas_call(
        functools.partial(add_core_kernel, planes),
        out_shape=[
            vmem_out((planes,) + shape, jnp.float32),
            vmem_out((planes,) + shape, jnp.bfloat16),
        ],
        in_specs=[VMEM] * 2,
        out_specs=[VMEM] * 2,
        compiler_params=params(2),
        name="add_core",
    )(keep, got)


def add_row_kernel(planes, stay, got, *outs):
    outs[0][...] = stay[0] + got[0].astype(jnp.float32)
    for k in range(1, planes):
        outs[k][...] = (stay[k] + got[k].astype(jnp.float32)).astype(outs[k].dtype)


def add_row(stay, got, planes):
    shape = stay.shape[1:]
    return pl.pallas_call(
        functools.partial(add_row_kernel, planes),
        out_shape=[vmem_out(shape, jnp.float32)]
        + [vmem_out(shape, jnp.bfloat16) for _ in range(planes - 1)],
        in_specs=[VMEM] * 2,
        out_specs=[VMEM] * planes,
        compiler_params=params(2),
        name="add_row",
    )(stay, got)


def finish_kernel(state, rows_row, mine, *refs):
    out = refs[-1]
    total = state[...] + mine[...]
    for got in refs[:-1]:
        total = total + got[...].astype(jnp.float32)
    requests = total.shape[0]
    numbers = lax.broadcasted_iota(jnp.int32, (requests, requests), 0)
    pick = (rows_row[...] == numbers).astype(jnp.bfloat16)
    out[...] = jnp.dot(
        pick, total.astype(jnp.bfloat16), preferred_element_type=jnp.float32
    ).astype(out.dtype)


def finish(state, rows_row, mine, got):
    return pl.pallas_call(
        finish_kernel,
        out_shape=jax.ShapeDtypeStruct(state.shape, jnp.bfloat16),
        in_specs=[VMEM] * (3 + len(got)),
        out_specs=VMEM,
        compiler_params=params(2),
        name="finish",
    )(state, rows_row, mine, *got)


def gather(message, size, planes, first_fill, second_fill):
    shifted = [shift(message, size, 4 * k) for k in range(1, planes)]
    fills = first_fill(message)
    b0 = stack([message] + shifted, fills)
    b1 = swap(b0, size, 2)
    c0 = swap(b0, size, 1)
    between = second_fill(b0, c0)
    c1 = swap(b1, size, 1)
    return b0, c0, b1, c1, fills, between


def on_device(size, *args):
    return layer_on_device(size, *args)


def layer_on_device(size, queries, keys_cache, values_cache, new_keys, new_values, lengths, assignment,
              residual, w_out, w_gate, w_up, w_down, norm_gain):
    planes = size // 4
    kv_heads = w_out.shape[1] // (queries.shape[2] * queries.shape[3])
    count = w_gate.shape[0] // ROWS
    meta = lax.axis_index("wide").astype(jnp.int32).reshape(1)
    requests = assignment.shape[0]
    att, wo = attention(
        meta, lengths, queries[0], keys_cache[0], values_cache[0], new_keys[0], new_values[0],
        w_out, kv_heads,
    )
    order = [(0, j) for j in range(count)] + [(1, j) for j in range(count)]
    ready = 2
    early = order[: count + ready]
    plans = [early[0:1], early[1:3], early[3:4], early[4:6], early[6:7]]
    weights = (w_gate, w_up)
    pieces = []

    b0, c0, b1, c1, f0, f1 = gather(
        att, size, planes,
        lambda m: prefetch(weights, plans[0], [m]),
        lambda b, c: prefetch(weights, plans[1], [b]),
    )
    f2 = prefetch(weights, plans[2], [b1, f1[0]])
    outs = project(
        meta, (b0, b1, c0, c1), wo, residual, assignment.reshape(1, requests),
        norm_gain.reshape(1, -1), weights, plans[3], [f2[0]], planes, kv_heads,
    )
    f3, (state, message) = outs[: len(plans[3])], outs[len(plans[3]) :]
    pieces = list(f0) + list(f1) + list(f2) + list(f3)

    def second_fill(b, c):
        return first_half(
            meta, b, c, pieces[:count], pieces[count:], w_up, w_down, planes
        )

    def first_fill(m):
        got = prefetch(weights, plans[4], [m])
        pieces.extend(got)
        return got

    b0, c0, b1, c1, _, outs = gather(message, size, planes, first_fill, second_fill)
    downs, (gate_sum, up_sum) = outs[:-2], outs[-2:]
    keep, send = second_half(
        meta, (b0, c0, b1, c1), gate_sum, up_sum, pieces[:count], pieces[count:], downs,
        w_up, w_down, planes,
    )
    stay, send = add_core(keep, swap(send, size, 1), planes)
    parts = add_row(stay, swap(send, size, 2), planes)
    got = [shift(parts[k], size, 4 * k) for k in range(1, planes)]
    return finish(state, assignment.reshape(1, requests), parts[0], got)


def masked_scores(query_rows, keys_local, lens_local, block_index, inv_scale):
    key_block = lax.dynamic_slice_in_dim(keys_local, block_index * KEY_BLOCK, KEY_BLOCK, 1)
    scores = (
        jnp.einsum("rqe,rpe->rqp", query_rows, key_block, preferred_element_type=jnp.float32)
        * inv_scale
    )
    position = block_index * KEY_BLOCK + lax.broadcasted_iota(jnp.int32, scores.shape, 2)
    return jnp.where(position < lens_local[:, None, None], scores, NEG_FILL)


def plain_on_device(
    queries,
    keys_cache,
    values_cache,
    new_keys,
    new_values,
    lengths,
    assignment,
    residual,
    w_out,
    w_gate,
    w_up,
    w_down,
    norm_gain,
):
    kv_heads = w_out.shape[1] // (queries.shape[2] * queries.shape[3])
    my_index = lax.axis_index("wide")
    my_shard = my_index // kv_heads
    req_dev = queries.shape[1]
    query_rows = queries[0]
    keys_local = keys_cache[0]
    values_local = values_cache[0]
    lens_local = lax.dynamic_slice_in_dim(lengths, my_shard * req_dev, req_dev)
    inv_scale = 1.0 / math.sqrt(query_rows.shape[2])
    own_score = (
        jnp.einsum("rqe,re->rq", query_rows, new_keys[0], preferred_element_type=jnp.float32)
        * inv_scale
    )
    block_count = (jnp.max(lens_local) + KEY_BLOCK - 1) // KEY_BLOCK

    def find_top(block_index, running):
        return jnp.maximum(
            running,
            jnp.max(
                masked_scores(query_rows, keys_local, lens_local, block_index, inv_scale), axis=2
            ),
        )

    top_score = lax.fori_loop(0, block_count, find_top, own_score)
    own_weight = jnp.exp(own_score - top_score)
    own_low = lax.optimization_barrier(own_weight.astype(jnp.bfloat16)).astype(jnp.float32)
    start_state = (own_weight, own_low[:, :, None] * new_values[0].astype(jnp.float32)[:, None, :])

    def accumulate(block_index, state_pair):
        total_sum, weighted = state_pair
        weights = jnp.exp(
            masked_scores(query_rows, keys_local, lens_local, block_index, inv_scale)
            - top_score[:, :, None]
        )
        value_block = lax.dynamic_slice_in_dim(values_local, block_index * KEY_BLOCK, KEY_BLOCK, 1)
        weighted = weighted + jnp.einsum(
            "rqp,rpe->rqe",
            weights.astype(jnp.bfloat16),
            value_block,
            preferred_element_type=jnp.float32,
        )
        return (total_sum + jnp.sum(weights, axis=2), weighted)

    total_sum, weighted = lax.fori_loop(0, block_count, accumulate, start_state)
    attended = (weighted / total_sum[:, :, None]).astype(jnp.bfloat16).reshape(1, req_dev, -1)
    feat_width = attended.shape[2]
    head_piece = lax.all_gather(attended, "wide", axis=0, tiled=True)

    def one_source(offset, running):
        source_shard = offset // kv_heads
        source_group = offset % kv_heads
        request_ids = lax.dynamic_slice_in_dim(assignment, source_shard * req_dev, req_dev)
        out_cols = lax.dynamic_slice_in_dim(w_out, source_group * feat_width, feat_width, 1)
        source_rows = lax.dynamic_index_in_dim(head_piece, offset, 0, keepdims=False)
        term = contract_last(source_rows, out_cols)
        return running.at[request_ids].add(term)

    projected = lax.fori_loop(
        0,
        head_piece.shape[0],
        one_source,
        jnp.zeros((assignment.shape[0], w_out.shape[0]), jnp.float32),
    )
    hidden_state = residual.astype(jnp.float32) + projected
    row_squares = lax.psum(jnp.sum(hidden_state * hidden_state, axis=1), "wide")
    inv_rms = lax.rsqrt(row_squares / w_out.shape[1] + EPSILON)
    normed_cols = (hidden_state * inv_rms[:, None] * norm_gain[None, :]).astype(jnp.bfloat16)
    normed_piece = lax.all_gather(normed_cols, "wide", axis=1, tiled=True)
    gate_val = contract_last(normed_piece, w_gate)
    up_val = contract_last(normed_piece, w_up)
    activated = (jax.nn.silu(gate_val) * up_val).astype(jnp.bfloat16)
    down_terms = jnp.dot(activated, w_down, preferred_element_type=jnp.float32)
    down_part = lax.psum_scatter(down_terms, "wide", scatter_dimension=1, tiled=True)
    return (hidden_state + down_part).astype(jnp.bfloat16)


def fits(size, w_out, w_gate):
    features, units = w_out.shape[0] // size, w_gate.shape[0] // size
    resident = 2 * units * w_gate.shape[1] * 2
    return (
        size % 4 == 0
        and features % LANES == 0
        and units % ROWS == 0
        and units // ROWS >= 5
        and resident <= 44 << 20
    )


def solution(mesh):
    size = mesh.shape["wide"]
    placed = (
        P(("groups", "wide"), None, None, None),
        P(("groups", "wide"), None, None, None),
        P(("groups", "wide"), None, None, None),
        P(("groups", "wide"), None, None),
        P(("groups", "wide"), None, None),
        P("groups"),
        P("groups"),
        P("groups", "wide"),
        P("wide", None),
        P("wide", None),
        P("wide", None),
        P("wide", None),
        P("wide"),
    )

    def sharded(body):
        return jax.shard_map(
            body, mesh=mesh, in_specs=placed, out_specs=P("groups", "wide"), check_vma=False
        )

    fast = sharded(functools.partial(on_device, size))
    plain = sharded(plain_on_device)

    def layer(*args):
        return (fast if fits(size, args[8], args[9]) else plain)(*args)

    return layer
```
